768 devices in a mesh: dp: 8 (over x, core), segment: 8 (over y), seq: 12 (over z).
Axes of the slice: x: 4, y: 8, z: 12, core: 2. Of those that a mesh axis runs over, the one named last changes fastest.
Arguments:
- activations: bfloat16 [8, 4, 1536, 768], P('dp', None, 'seq'), may hold values from -6 to 6
- conv_weight: bfloat16 [8, 5, 768, 768], P('segment', None, ('dp', 'seq')), may hold values from -0.125 to 0.125
- norm_gain: float32 [8, 768], P('segment'), may hold values from 0.25 to 1.75
- conv_bias: float32 [8, 768], P('segment'), may hold values from -3 to 3
Outputs:
- block_outputs: bfloat16 [8, 8, 4, 1536, 768], P('segment', 'dp', None, 'seq')
The draws below stay inside these ranges and needn't reach their ends.
All inputs are finite; a program needn't handle non-finite values.
Results may differ from the reference program's by a relative error of at most 0.0065.
Values may be sent and summed in bfloat16 or wider, within the bound.
No kernel may reach another device: no remote copies, remote signals or barrier semaphores. Data moves between devices by JAX's collectives and lax.ppermute only.
A program may use at most 32 MiB of HBM per device.

```python
import jax
import jax.numpy as jnp
from jax import lax

C = 768
KW = 5
M = 4
L = 1536
BATCH = 8
SEGMENTS = 8


def block_scale(stream_key, dims, shards, smallest, high):
    loudness, own = 1.0, jax.random.fold_in(stream_key, 6)
    for axis_at, blocks in shards:
        steps = jnp.exp(jax.random.uniform(jax.random.fold_in(own, axis_at), (blocks,), jnp.float32, smallest / len(shards), high / len(shards)))
        loudness = loudness * jnp.repeat(steps, dims[axis_at] // blocks).reshape([-1 if axis == axis_at else 1 for axis in range(len(dims))])
    return loudness


def gaussian(stream_key, extent, width, limit, split=(), held_as=jnp.bfloat16):
    array = width * jax.random.normal(stream_key, extent, jnp.float32)
    if split:
        array = array * block_scale(stream_key, extent, split, -0.22, 0.18)
    return jnp.clip(array, -limit, limit).astype(held_as)


def setup_inputs(seed: int = 0) -> dict:
    key_of = jax.random.split(jax.random.key(seed), 5)
    activations = gaussian(key_of[0], (BATCH, M, L, C), 1.0, 6.0, ((0, 8), (2, 12)))
    conv_weight = gaussian(key_of[1], (SEGMENTS, KW, C, C), (KW * C // 2) ** -0.5, 0.125, ((0, 8), (2, 96)))
    norm_gain = jnp.clip(1.0 + 0.15 * jax.random.normal(key_of[2], (SEGMENTS, C), jnp.float32), 0.25, 1.75)
    conv_bias = gaussian(key_of[3], (SEGMENTS, C), 0.5, 3.0, ((0, 8),), jnp.float32)
    return {"activations": activations, "conv_weight": conv_weight, "norm_gain": norm_gain, "conv_bias": conv_bias}


def block(rows, weight, gain, bias):
    wide = rows.astype(jnp.float32)
    stat = lax.optimization_barrier(jnp.mean(wide * wide, axis=-1, keepdims=True))
    normed = (wide / jnp.sqrt(stat + 1e-06) * gain).astype(jnp.bfloat16)
    padded = jnp.pad(normed, ((2, 2), (0, 0)))
    length = rows.shape[0]
    total = jnp.zeros((length, weight.shape[2]), jnp.float32)
    for tap in range(KW):
        total = total + jnp.dot(padded[tap:tap + length], weight[tap], preferred_element_type=jnp.float32)
    return wide + jax.nn.gelu(total + bias, approximate=True)

def reference(activations, conv_weight, norm_gain, conv_bias):
    results = []
    for segment in range(SEGMENTS):
        results.append([])
    for slot in range(BATCH):
        for micro in range(M):
            current = activations[slot, micro]
            first = None
            for segment in range(SEGMENTS):
                lifted = block(current, conv_weight[segment], norm_gain[segment], conv_bias[segment])
                if segment == SEGMENTS - 1:
                    final = (lifted + first.astype(jnp.float32)).astype(jnp.bfloat16)
                    results[segment].append(final)
                else:
                    current = lifted.astype(jnp.bfloat16)
                    if segment == 0:
                        first = current
                    results[segment].append(current)
    stacked = [jnp.stack(items).reshape(BATCH, M, L, C) for items in results]
    return jnp.stack(stacked)
```

```python
import jax
import jax.numpy as jnp
from jax import lax
from jax.experimental import pallas as pl
from jax.experimental.pallas import tpu as pltpu
from jax.sharding import Mesh, PartitionSpec as P

PAIR = 2


def shifted(block, axis, distance):
    count = lax.axis_size(axis)
    return lax.ppermute(block, axis, [(i, (i + distance) % count) for i in range(count)])


def moved(block, axis, distance):
    devices = range(lax.axis_size(axis))
    return lax.ppermute(block, axis, [(i, i + distance) for i in devices if i + distance in devices])


def assemble_kernel(pieces, taps, group, where_ref, *refs):
    sources, target, sems = refs[: len(pieces)], refs[-2], refs[-1]
    copies = []
    for at, (row, first, count) in enumerate(pieces):
        base = where_ref[row] * group + first
        for tap in range(taps):
            copies.append(
                pltpu.make_async_copy(
                    sources[at].at[:, tap],
                    target.at[tap, pl.ds(base, count)],
                    sems.at[at * taps + tap],
                )
            )
    for copy in copies:
        copy.start()
    for copy in copies:
        copy.wait()


def gathered(shard):
    taps, rows, width = shard.shape
    group = lax.axis_size("seq")
    half = group // 2
    across = lax.axis_size("x")
    own = lax.all_gather(shard.reshape(1, taps * rows, width), "seq", axis=0, tiled=True)
    low, high = own[:half], own[half:]
    left_low, left_high = shifted(low, "x", 1), shifted(high, "x", 1)
    right_high, right_low = shifted(high, "x", -1), shifted(low, "x", -1)
    far_low, far_high = shifted(left_low, "x", 1), shifted(right_high, "x", -1)
    mine = [
        (own, 0, 0, group),
        (left_low, -1, 0, half),
        (left_high, -1, half, half),
        (right_low, 1, 0, half),
        (right_high, 1, half, half),
        (far_low, 2, 0, half),
        (far_high, 2, half, half),
    ]
    x, core = lax.axis_index("x"), lax.axis_index("core")
    arrays, pieces, rows_of = [], [], []
    for other in range(2):
        for block, offset, first, count in mine:
            array = shifted(block, "core", 1) if other else block
            arrays.append(array.reshape(count, taps, rows, width))
            pieces.append((len(rows_of), first, count))
            holder = core if not other else 1 - core
            rows_of.append(((x + offset + across) % across) * 2 + holder)
    where = jnp.stack(rows_of).astype(jnp.int32)
    blocks = across * 2 * group
    out = pl.pallas_call(
        lambda *refs: assemble_kernel(pieces, taps, group, *refs),
        out_shape=jax.ShapeDtypeStruct((taps, blocks, rows, width), shard.dtype),
        in_specs=[pl.BlockSpec(memory_space=pltpu.SMEM)]
        + [pl.BlockSpec(memory_space=pl.ANY)] * len(arrays),
        out_specs=pl.BlockSpec(memory_space=pltpu.VMEM),
        scratch_shapes=[pltpu.SemaphoreType.DMA((len(pieces) * taps,))],
        compiler_params=pltpu.CompilerParams(vmem_limit_bytes=16 << 20),
        name="assemble",
    )(where, *arrays)
    return out.reshape(taps * blocks * rows, width)


def block_kernel(taps, length, halo, has_own, has_incoming, has_join, info_ref, *refs):
    refs = list(refs)
    incoming_ref = refs.pop(0) if has_incoming else None
    own_ref = refs.pop(0) if has_own else None
    join_ref = refs.pop(0) if has_join else None
    kernel_ref, gain_ref, bias_ref, out_ref, cat_ref = refs
    extent, width = out_ref.shape

    @pl.when(info_ref[0] == 1)
    def _():
        if has_own and has_incoming:
            pick = info_ref[2] == 1
            wide = jnp.where(pick, own_ref[...].astype(jnp.float32), incoming_ref[...].astype(jnp.float32))
        else:
            wide = (own_ref if has_own else incoming_ref)[...].astype(jnp.float32)
        stat = jnp.mean(wide * wide, axis=-1, keepdims=True)
        place = info_ref[1] + lax.broadcasted_iota(jnp.int32, (extent, 1), 0)
        inside = jnp.logical_and(place >= 0, place < length)
        normed = wide * lax.rsqrt(stat + 1e-06) * gain_ref[...]
        normed = jnp.where(inside, normed, 0.0)
        for tap in range(taps):
            back = (taps // 2 - tap) % extent
            turned = pltpu.roll(normed, back, 0) if back else normed
            cat_ref[:, tap * width : (tap + 1) * width] = turned.astype(jnp.bfloat16)
        total = jnp.dot(cat_ref[...], kernel_ref[...], preferred_element_type=jnp.float32)
        lifted = wide + jax.nn.gelu(total + bias_ref[...], approximate=True)
        out_ref[...] = lifted.astype(jnp.bfloat16)
        if has_join:

            @pl.when(info_ref[3] == 1)
            def _():
                inner = lifted[halo : extent - halo] + join_ref[...].astype(jnp.float32)
                out_ref[halo : extent - halo, :] = inner.astype(jnp.bfloat16)


def block(info, incoming, own, join, kernel, gain, bias, taps, length, halo):
    given = [a for a in (incoming, own, join) if a is not None]
    extent, width = (incoming if incoming is not None else own).shape
    vmem = pl.BlockSpec(memory_space=pltpu.VMEM)
    return pl.pallas_call(
        lambda *refs: block_kernel(
            taps, length, halo, own is not None, incoming is not None, join is not None, *refs
        ),
        out_shape=jax.ShapeDtypeStruct((extent, width), jnp.bfloat16),
        in_specs=[pl.BlockSpec(memory_space=pltpu.SMEM)] + [vmem] * (len(given) + 3),
        out_specs=vmem,
        scratch_shapes=[pltpu.VMEM((extent, taps * width), jnp.bfloat16)],
        compiler_params=pltpu.CompilerParams(vmem_limit_bytes=16 << 20),
        cost_estimate=pl.CostEstimate(
            flops=2 * extent * taps * width * width,
            bytes_accessed=2 * taps * width * width,
            transcendentals=extent * width,
        ),
        name="block",
    )(info, *given, kernel, gain, bias)


def per_device(activations, conv_weight, norm_gain, conv_bias):
    inputs = activations[0]
    micro_count, rows, width = inputs.shape
    segments = lax.axis_size("segment")
    segment = lax.axis_index("segment")
    seq = lax.axis_index("seq")
    taps = conv_weight.shape[1]
    halo = segments * (taps // 2)
    length = rows * lax.axis_size("seq")

    before = moved(inputs[:, rows - halo :], "seq", 1)
    after = moved(inputs[:, :halo], "seq", -1)
    extended = jnp.concatenate([before, inputs, after], axis=1)
    kernel = gathered(conv_weight[0])

    pairs = micro_count // PAIR
    turns = segments + pairs - 1
    start = seq * rows - halo
    last = (segment == segments - 1).astype(jnp.int32)
    first = (segment == 0).astype(jnp.int32)
    incoming = [None] * PAIR
    kept = [None] * micro_count
    early = []
    joined = None
    for turn in range(turns):
        pair = turn - segment
        valid = jnp.logical_and(pair >= 0, pair < pairs).astype(jnp.int32)
        info = jnp.stack([valid, start, first, last]).astype(jnp.int32)
        for lane in range(PAIR):
            own = extended[turn * PAIR + lane] if turn < pairs else None
            join = joined[(turn - segments + 1) * PAIR + lane] if turn >= segments - 1 else None
            out = block(info, incoming[lane], own, join, kernel, norm_gain, conv_bias, taps, length, halo)
            if turn < turns - 1:
                incoming[lane] = moved(out, "segment", 1)
            inner = out[halo : halo + rows]
            if turn < pairs:
                early.append(inner)
            for which in range(pairs):
                if which <= turn < segments + which:
                    at = which * PAIR + lane
                    kept[at] = inner if kept[at] is None else jnp.where(pair == which, inner, kept[at])
        if turn == pairs - 1:
            joined = lax.ppermute(jnp.stack(early), "segment", [(0, segments - 1)])
    return jnp.stack(kept)[None, None]


def solution(mesh):
    dp, segments, seq = (mesh.shape[name] for name in ("dp", "segment", "seq"))
    split = Mesh(mesh.devices.reshape(dp // 2, 2, segments, seq), ("x", "core", "segment", "seq"))
    in_specs = (
        P(("x", "core"), None, "seq", None),
        P("segment", None, ("x", "core", "seq"), None),
        P("segment", None),
        P("segment", None),
    )
    out_specs = P("segment", ("x", "core"), None, "seq", None)
    return jax.shard_map(
        per_device, mesh=split, in_specs=in_specs, out_specs=out_specs, check_vma=False
    )
```

```python
import jax
import jax.numpy as jnp
from jax import lax
from jax.experimental import pallas as pl
from jax.experimental.pallas import tpu as pltpu
from jax.sharding import Mesh, PartitionSpec as P


PAIR = 2


def shifted(block, axis, distance):
    count = lax.axis_size(axis)
    return lax.ppermute(block, axis, [(i, (i + distance) % count) for i in range(count)])


def moved(block, axis, distance):
    devices = range(lax.axis_size(axis))
    return lax.ppermute(block, axis, [(i, i + distance) for i in devices if i + distance in devices])


def merge_kernel(counts, *refs):
    sources, target, sems = refs[:-2], refs[-2], refs[-1]
    copies, at = [], 0
    for index, count in enumerate(counts):
        copies.append(pltpu.make_async_copy(sources[index], target.at[at : at + count], sems.at[index]))
        at += count
    for copy in copies:
        copy.start()
    for copy in copies:
        copy.wait()


def merged(blocks):
    counts = [block.shape[0] for block in blocks]
    return pl.pallas_call(
        lambda *refs: merge_kernel(counts, *refs),
        out_shape=jax.ShapeDtypeStruct((sum(counts),) + blocks[0].shape[1:], blocks[0].dtype),
        in_specs=[pl.BlockSpec(memory_space=pl.ANY)] * len(blocks),
        out_specs=pl.BlockSpec(memory_space=pltpu.VMEM),
        scratch_shapes=[pltpu.SemaphoreType.DMA((len(blocks),))],
        compiler_params=pltpu.CompilerParams(vmem_limit_bytes=8 << 20),
        name="merge",
    )(*blocks)


def assemble_kernel(pieces, taps, group, where_ref, *refs):
    sources, target, sems = refs[:-2], refs[-2], refs[-1]
    copies = []
    for at, (source, skip, row, first, count) in enumerate(pieces):
        base = where_ref[row] * group + first
        for tap in range(taps):
            copies.append(
                pltpu.make_async_copy(
                    sources[source].at[skip : skip + count, tap],
                    target.at[tap, pl.ds(base, count)],
                    sems.at[at * taps + tap],
                )
            )
    for copy in copies:
        copy.start()
    for copy in copies:
        copy.wait()


def gathered(shard, places):
    taps, rows, width = shard.shape
    group = lax.axis_size("seq")
    half = group // 2
    across = lax.axis_size("x")
    own = lax.all_gather(shard.reshape(1, taps * rows, width), "seq", axis=0, tiled=True)
    low, high = own[:half], own[half:]
    left_low, left_high = shifted(low, "x", 1), shifted(high, "x", 1)
    right_high, right_low = shifted(high, "x", -1), shifted(low, "x", -1)
    far_low = shifted(left_low, "x", 1)
    far_high = shifted(right_high, "x", -1)
    parts = [
        (own, 0, 0),
        (left_low, 3, 0),
        (left_high, 3, half),
        (right_low, 1, 0),
        (right_high, 1, half),
        (far_low, 2, 0),
        (far_high, 2, half),
    ]
    arrays, pieces = [], []
    for block, offset, first in parts:
        pieces.append((len(arrays), 0, offset, first, block.shape[0]))
        arrays.append(block)
    for some in (parts[:5], parts[5:]):
        skip = 0
        for block, offset, first in some:
            pieces.append((len(arrays), skip, across + offset, first, block.shape[0]))
            skip += block.shape[0]
        both = merged([part[0] for part in some])
        arrays.append(shifted(both, "core", 1))
    blocks = across * 2 * group
    out = pl.pallas_call(
        lambda *refs: assemble_kernel(pieces, taps, group, *refs),
        out_shape=jax.ShapeDtypeStruct((taps, blocks, rows, width), shard.dtype),
        in_specs=[pl.BlockSpec(memory_space=pltpu.SMEM)]
        + [pl.BlockSpec(memory_space=pl.ANY)] * len(arrays),
        out_specs=pl.BlockSpec(memory_space=pltpu.VMEM),
        scratch_shapes=[pltpu.SemaphoreType.DMA((len(pieces) * taps,))],
        compiler_params=pltpu.CompilerParams(vmem_limit_bytes=16 << 20),
        name="assemble",
    )(places, *[array.reshape(-1, taps, rows, width) for array in arrays])
    return out.reshape(taps * blocks * rows, width)


def block_kernel(turn, pairs, segments, taps, length, halo, has_own, has_incoming, has_join, info_ref, *refs):
    refs = list(refs)
    incoming_ref = refs.pop(0) if has_incoming else None
    own_ref = refs.pop(0) if has_own else None
    join_ref = refs.pop(0) if has_join else None
    kernel_ref, gain_ref, bias_ref, out_ref, cat_ref = refs
    extent, width = out_ref.shape
    segment = info_ref[0]
    pair = turn - segment

    @pl.when(jnp.logical_and(pair >= 0, pair < pairs))
    def _():
        if has_own and has_incoming:
            pick = segment == 0
            wide = jnp.where(pick, own_ref[...].astype(jnp.float32), incoming_ref[...].astype(jnp.float32))
        else:
            wide = (own_ref if has_own else incoming_ref)[...].astype(jnp.float32)
        stat = jnp.mean(wide * wide, axis=-1, keepdims=True)
        place = info_ref[1] + lax.broadcasted_iota(jnp.int32, (extent, 1), 0)
        inside = jnp.logical_and(place >= 0, place < length)
        normed = wide * lax.rsqrt(stat + 1e-06) * gain_ref[...]
        normed = jnp.where(inside, normed, 0.0)
        for tap in range(taps):
            back = (taps // 2 - tap) % extent
            turned = pltpu.roll(normed, back, 0) if back else normed
            cat_ref[:, tap * width : (tap + 1) * width] = turned.astype(jnp.bfloat16)
        total = jnp.dot(cat_ref[...], kernel_ref[...], preferred_element_type=jnp.float32)
        lifted = wide + jax.nn.gelu(total + bias_ref[...], approximate=True)
        out_ref[...] = lifted.astype(jnp.bfloat16)
        if has_join:

            @pl.when(segment == segments - 1)
            def _():
                inner = lifted[halo : extent - halo] + join_ref[...].astype(jnp.float32)
                out_ref[halo : extent - halo, :] = inner.astype(jnp.bfloat16)


def block(info, incoming, own, join, kernel, gain, bias, turn, pairs, segments, taps, length, halo):
    given = [a for a in (incoming, own, join) if a is not None]
    extent, width = (incoming if incoming is not None else own).shape
    vmem = pl.BlockSpec(memory_space=pltpu.VMEM)
    return pl.pallas_call(
        lambda *refs: block_kernel(
            turn, pairs, segments, taps, length, halo, own is not None, incoming is not None, join is not None, *refs
        ),
        out_shape=jax.ShapeDtypeStruct((extent, width), jnp.bfloat16),
        in_specs=[pl.BlockSpec(memory_space=pltpu.SMEM)] + [vmem] * (len(given) + 3),
        out_specs=vmem,
        scratch_shapes=[pltpu.VMEM((extent, taps * width), jnp.bfloat16)],
        compiler_params=pltpu.CompilerParams(vmem_limit_bytes=16 << 20),
        cost_estimate=pl.CostEstimate(
            flops=2 * extent * taps * width * width,
            bytes_accessed=2 * taps * width * width,
            transcendentals=extent * width,
        ),
        name="block",
    )(info, *given, kernel, gain, bias)


def per_device(activations, conv_weight, norm_gain, conv_bias):
    inputs = activations[0]
    micro_count, rows, _ = inputs.shape
    segments = lax.axis_size("segment")
    segment = lax.axis_index("segment")
    seq = lax.axis_index("seq")
    taps = conv_weight.shape[1]
    halo = segments * (taps // 2)
    length = rows * lax.axis_size("seq")

    before = moved(inputs[:, rows - halo :], "seq", 1)
    after = moved(inputs[:, :halo], "seq", -1)
    extended = jnp.concatenate([before, inputs, after], axis=1)
    pairs = micro_count // PAIR
    turns = segments + pairs - 1
    x, core, across = lax.axis_index("x"), lax.axis_index("core"), lax.axis_size("x")
    order = lax.rem(x + jnp.arange(across, dtype=jnp.int32), across) * 2
    places = jnp.concatenate([order + core, order + 1 - core])
    info = jnp.stack([segment, seq * rows - halo]).astype(jnp.int32)
    owns = [[turn - segment == which for turn in range(turns)] for which in range(pairs)]
    owns, info, places, shard = lax.optimization_barrier((owns, info, places, conv_weight[0]))
    kernel = gathered(shard, places)
    incoming = [None] * PAIR
    kept = [None] * micro_count
    early = []
    joined = None
    for turn in range(turns):
        for lane in range(PAIR):
            own = extended[turn * PAIR + lane] if turn < pairs else None
            join = joined[(turn - segments + 1) * PAIR + lane] if turn >= segments - 1 else None
            out = block(info, incoming[lane], own, join, kernel, norm_gain, conv_bias, turn, pairs, segments, taps, length, halo)
            if turn < turns - 1:
                incoming[lane] = moved(out, "segment", 1)
            inner = out[halo : halo + rows]
            if turn < pairs:
                early.append(inner)
            for which in range(pairs):
                if which <= turn < segments + which:
                    at = which * PAIR + lane
                    kept[at] = inner if kept[at] is None else jnp.where(owns[which][turn], inner, kept[at])
        if turn == pairs - 1:
            joined = lax.ppermute(jnp.stack(early), "segment", [(0, segments - 1)])
    return jnp.stack(kept)[None, None]


def solution(mesh):
    dp, segments, seq = (mesh.shape[name] for name in ("dp", "segment", "seq"))
    split = Mesh(mesh.devices.reshape(dp // 2, 2, segments, seq), ("x", "core", "segment", "seq"))
    in_specs = (
        P(("x", "core"), None, "seq", None),
        P("segment", None, ("x", "core", "seq"), None),
        P("segment", None),
        P("segment", None),
    )
    out_specs = P("segment", ("x", "core"), None, "seq", None)

    return jax.shard_map(per_device, mesh=split, in_specs=in_specs, out_specs=out_specs, check_vma=False)
```

```python
import jax
import jax.numpy as jnp
from jax import lax
from jax.experimental import pallas as pl
from jax.experimental.pallas import tpu as pltpu
from jax.sharding import Mesh, PartitionSpec as P


PAIR = 2


def shifted(block, axis, distance):
    count = lax.axis_size(axis)
    return lax.ppermute(block, axis, [(i, (i + distance) % count) for i in range(count)])


def moved(block, axis, distance):
    devices = range(lax.axis_size(axis))
    return lax.ppermute(block, axis, [(i, i + distance) for i in devices if i + distance in devices])


def merge_kernel(counts, *refs):
    sources, target, sems = refs[:-2], refs[-2], refs[-1]
    copies, at = [], 0
    for index, count in enumerate(counts):
        copies.append(pltpu.make_async_copy(sources[index], target.at[at : at + count], sems.at[index]))
        at += count
    for copy in copies:
        copy.start()
    for copy in copies:
        copy.wait()


def merged(blocks):
    counts = [block.shape[0] for block in blocks]
    return pl.pallas_call(
        lambda *refs: merge_kernel(counts, *refs),
        out_shape=jax.ShapeDtypeStruct((sum(counts),) + blocks[0].shape[1:], blocks[0].dtype),
        in_specs=[pl.BlockSpec(memory_space=pl.ANY)] * len(blocks),
        out_specs=pl.BlockSpec(memory_space=pltpu.VMEM),
        scratch_shapes=[pltpu.SemaphoreType.DMA((len(blocks),))],
        compiler_params=pltpu.CompilerParams(vmem_limit_bytes=8 << 20),
        name="merge",
    )(*blocks)


def assemble_kernel(pieces, taps, group, where_ref, *refs):
    sources, target, sems = refs[:-2], refs[-2], refs[-1]
    copies = []
    for at, (source, skip, row, first, count) in enumerate(pieces):
        base = where_ref[row] * group + first
        for tap in range(taps):
            copies.append(
                pltpu.make_async_copy(
                    sources[source].at[skip : skip + count, tap],
                    target.at[tap, pl.ds(base, count)],
                    sems.at[at * taps + tap],
                )
            )
    for copy in copies:
        copy.start()
    for copy in copies:
        copy.wait()


def gathered(shard, places):
    taps, rows, width = shard.shape
    group = lax.axis_size("seq")
    half = group // 2
    across = lax.axis_size("x")
    own = lax.all_gather(shard.reshape(1, taps * rows, width), "seq", axis=0, tiled=True)
    low, high = own[:half], own[half:]
    left_low, left_high = shifted(low, "x", 1), shifted(high, "x", 1)
    right_high, right_low = shifted(high, "x", -1), shifted(low, "x", -1)
    far_low = shifted(left_low, "x", 1)
    far_high = shifted(right_high, "x", -1)
    parts = [
        (own, 0, 0),
        (left_low, 3, 0),
        (left_high, 3, half),
        (right_low, 1, 0),
        (right_high, 1, half),
        (far_low, 2, 0),
        (far_high, 2, half),
    ]
    arrays, pieces = [], []
    for block, offset, first in parts:
        pieces.append((len(arrays), 0, offset, first, block.shape[0]))
        arrays.append(block)
    for some in (parts[:5], parts[5:]):
        skip = 0
        for block, offset, first in some:
            pieces.append((len(arrays), skip, across + offset, first, block.shape[0]))
            skip += block.shape[0]
        both = merged([part[0] for part in some])
        arrays.append(shifted(both, "core", 1))
    blocks = across * 2 * group
    out = pl.pallas_call(
        lambda *refs: assemble_kernel(pieces, taps, group, *refs),
        out_shape=jax.ShapeDtypeStruct((taps, blocks, rows, width), shard.dtype),
        in_specs=[pl.BlockSpec(memory_space=pltpu.SMEM)]
        + [pl.BlockSpec(memory_space=pl.ANY)] * len(arrays),
        out_specs=pl.BlockSpec(memory_space=pltpu.VMEM),
        scratch_shapes=[pltpu.SemaphoreType.DMA((len(pieces) * taps,))],
        compiler_params=pltpu.CompilerParams(vmem_limit_bytes=16 << 20),
        name="assemble",
    )(places, *[array.reshape(-1, taps, rows, width) for array in arrays])
    return out.reshape(taps * blocks * rows, width)


def block_kernel(turn, pairs, segments, taps, length, halo, trim, has_own, has_incoming, has_join, info_ref, *refs):
    refs = list(refs)
    incoming_ref = refs.pop(0) if has_incoming else None
    own_ref = refs.pop(0) if has_own else None
    join_ref = refs.pop(0) if has_join else None
    kernel_ref, gain_ref, bias_ref, out_ref, cat_ref = refs
    extent, width = cat_ref.shape[0], out_ref.shape[1]
    cut = (extent - out_ref.shape[0]) // 2
    segment = info_ref[0]
    pair = turn - segment

    @pl.when(jnp.logical_and(pair >= 0, pair < pairs))
    def _():
        if has_own and has_incoming:
            pick = segment == 0
            wide = jnp.where(pick, own_ref[...].astype(jnp.float32), incoming_ref[...].astype(jnp.float32))
        else:
            wide = (own_ref if has_own else incoming_ref)[...].astype(jnp.float32)
        stat = jnp.mean(wide * wide, axis=-1, keepdims=True)
        place = info_ref[1] + trim + lax.broadcasted_iota(jnp.int32, (extent, 1), 0)
        inside = jnp.logical_and(place >= 0, place < length)
        normed = wide * lax.rsqrt(stat + 1e-06) * gain_ref[...]
        normed = jnp.where(inside, normed, 0.0)
        for tap in range(taps):
            back = (taps // 2 - tap) % extent
            turned = pltpu.roll(normed, back, 0) if back else normed
            cat_ref[:, tap * width : (tap + 1) * width] = turned.astype(jnp.bfloat16)
        total = jnp.dot(cat_ref[...], kernel_ref[...], preferred_element_type=jnp.float32)
        lifted = wide + jax.nn.gelu(total + bias_ref[...], approximate=True)
        out_ref[...] = lifted[cut : extent - cut].astype(jnp.bfloat16)
        if has_join:

            @pl.when(segment == segments - 1)
            def _():
                inner = lifted[halo - trim : extent - halo + trim] + join_ref[...].astype(jnp.float32)
                edge = halo - trim - cut
                out_ref[edge : out_ref.shape[0] - edge, :] = inner.astype(jnp.bfloat16)


def block(info, incoming, own, join, kernel, gain, bias, turn, pairs, segments, taps, length, halo, trim, trim_out):
    given = [a for a in (incoming, own, join) if a is not None]
    extent, width = (incoming if incoming is not None else own).shape
    vmem = pl.BlockSpec(memory_space=pltpu.VMEM)
    return pl.pallas_call(
        lambda *refs: block_kernel(
            turn, pairs, segments, taps, length, halo, trim, own is not None, incoming is not None, join is not None, *refs
        ),
        out_shape=jax.ShapeDtypeStruct((extent - 2 * (trim_out - trim), width), jnp.bfloat16),
        in_specs=[pl.BlockSpec(memory_space=pltpu.SMEM)] + [vmem] * (len(given) + 3),
        out_specs=vmem,
        scratch_shapes=[pltpu.VMEM((extent, taps * width), jnp.bfloat16)],
        compiler_params=pltpu.CompilerParams(vmem_limit_bytes=16 << 20),
        cost_estimate=pl.CostEstimate(
            flops=2 * extent * taps * width * width,
            bytes_accessed=2 * taps * width * width,
            transcendentals=extent * width,
        ),
        name="block",
    )(info, *given, kernel, gain, bias)


def per_device(activations, conv_weight, norm_gain, conv_bias):
    inputs = activations[0]
    micro_count, rows, _ = inputs.shape
    segments = lax.axis_size("segment")
    segment = lax.axis_index("segment")
    seq = lax.axis_index("seq")
    taps = conv_weight.shape[1]
    halo = segments * (taps // 2)
    length = rows * lax.axis_size("seq")

    before = moved(inputs[:, rows - halo :], "seq", 1)
    after = moved(inputs[:, :halo], "seq", -1)
    extended = jnp.concatenate([before, inputs, after], axis=1)
    pairs = micro_count // PAIR
    turns = segments + pairs - 1
    x, core, across = lax.axis_index("x"), lax.axis_index("core"), lax.axis_size("x")
    order = lax.rem(x + jnp.arange(across, dtype=jnp.int32), across) * 2
    places = jnp.concatenate([order + core, order + 1 - core])
    info = jnp.stack([segment, seq * rows - halo]).astype(jnp.int32)
    owns = [[turn - segment == which for turn in range(turns)] for which in range(pairs)]
    owns, info, places, shard = lax.optimization_barrier((owns, info, places, conv_weight[0]))
    kernel = gathered(shard, places)
    incoming = [None] * PAIR
    kept = [None] * micro_count
    early = []
    joined = None
    trims = [max(0, turn - pairs + 1) * (taps // 2) // 8 * 8 for turn in range(turns)]
    for turn in range(turns):
        trim, trim_out = trims[turn], trims[min(turn + 1, turns - 1)]
        hops = [(s, s + 1) for s in range(segments - 1) if 0 <= turn - s < pairs]
        for lane in range(PAIR):
            own = extended[turn * PAIR + lane] if turn < pairs else None
            join = joined[(turn - segments + 1) * PAIR + lane] if turn >= segments - 1 else None
            out = block(info, incoming[lane], own, join, kernel, norm_gain, conv_bias, turn, pairs, segments, taps, length, halo, trim, trim_out)
            if turn < turns - 1:
                incoming[lane] = lax.ppermute(out, "segment", hops)
            inner = out[halo - trim_out : halo - trim_out + rows]
            if turn < pairs:
                early.append(inner)
            for which in range(pairs):
                if which <= turn < segments + which:
                    at = which * PAIR + lane
                    kept[at] = inner if kept[at] is None else jnp.where(owns[which][turn], inner, kept[at])
        if turn == pairs - 1:
            joined = lax.ppermute(jnp.stack(early), "segment", [(0, segments - 1)])
    return jnp.stack(kept)[None, None]


def solution(mesh):
    dp, segments, seq = (mesh.shape[name] for name in ("dp", "segment", "seq"))
    split = Mesh(mesh.devices.reshape(dp // 2, 2, segments, seq), ("x", "core", "segment", "seq"))
    in_specs = (
        P(("x", "core"), None, "seq", None),
        P("segment", None, ("x", "core", "seq"), None),
        P("segment", None),
        P("segment", None),
    )
    out_specs = P("segment", ("x", "core"), None, "seq", None)

    return jax.shard_map(per_device, mesh=split, in_specs=in_specs, out_specs=out_specs, check_vma=False)
```
